32 devices in a mesh: groups: 2 (over x), space: 8 (over z, y), beam: 2 (over core).
Axes of the slice: x: 2, y: 2, z: 4, core: 2. Of those that a mesh axis runs over, the one named last changes fastest.
Arguments:
- s_matrix: bfloat16 [4096, 256, 480], P(('groups', 'beam'), 'space'), parts along dimension 0, may hold values from -6 to 6
- beam_index: int32 [2048, 2], P('beam'), may hold values from -24 to 23, as said below
- beam_amp: float32 [2048], P('beam'), may hold values from 0.5 to 2
- beam_phase: float32 [2048], P('beam'), may hold values from -3.140625 to 3.140625
- positions: int32 [2, 384, 2], replicated, may hold values from 0 to 239
Outputs:
- intensities: float32 [4, 384, 256, 240], P('groups', ('space', 'beam')), parts along dimension 0
The draws below stay inside these ranges and needn't reach their ends.
There are 2 independent parts, one for each index of `groups`. The reference program is written for one: setup_inputs(seed, part) draws one part's arguments, and reference() takes and returns one part's arrays. A program takes and returns all parts, laid end to end along the dimension named above; an argument that names none is the same for every part. Nothing has to cross between parts.
Inputs may be any that keep to these rules, and one draw needn't show every extreme that they name: `beam_index`: no two beams have the same wave-vector.
All inputs are finite; a program needn't handle non-finite values.
Results may differ from the reference program's by a relative error of at most 0.0072.
Values may be sent and summed in bfloat16 or wider, within the bound.
No kernel may reach another device: no remote copies, remote signals or barrier semaphores. Data moves between devices by JAX's collectives and lax.ppermute only.
A program may use at most 192 MiB of HBM per device.

```python
import math
import jax
import jax.numpy as jnp
from jax import lax

NB = 2048
RY = 256
RX = 240
NBATCH = 2
P_SIZE = 384
N_BEAM = 2


def draw_beam_index(key, part):
    middle = jax.random.permutation(jax.random.fold_in(key, 11), jnp.arange(1, 2303, dtype=jnp.int32))
    cells = jnp.concatenate([jnp.array([0, 2303], dtype=jnp.int32), middle], 0)[:NB]
    order = jax.random.permutation(jax.random.fold_in(key, 12), jnp.arange(NB, dtype=jnp.int32))
    cells = cells[order]
    row_part = cells // 48 - 24
    col_part = cells % 48 - 24
    return jnp.stack([row_part, col_part], 1).astype(jnp.int32)


def with_ends(values, key, least, top_value):
    place = [jax.random.randint(jax.random.fold_in(key, axis), (), 0, length) for axis, length in enumerate(values.shape)]
    main_axis = values.shape.index(max(values.shape))
    neighbour = place[:main_axis] + [(place[main_axis] + 1) % values.shape[main_axis]] + place[main_axis + 1:]
    return values.at[tuple(place)].set(least).at[tuple(neighbour)].set(top_value)


def shard_levels(rng, extent, shards, smallest, top_value):
    def one(axis_at, blocks):
        heights = jax.random.uniform(jax.random.fold_in(jax.random.fold_in(rng, 6), axis_at), (blocks,), jnp.float32, smallest / len(shards), top_value / len(shards))
        return jnp.repeat(jnp.exp(heights), extent[axis_at] // blocks).reshape((-1,) + (1,) * (len(extent) - axis_at - 1))

    loudness = one(*shards[0])
    for cut in shards[1:]:
        loudness = loudness * one(*cut)
    return loudness


def scatter_about(key, dims, width, bound, shards=(), kind=jnp.bfloat16):
    drawn = jax.random.normal(key, dims, jnp.float32) * width
    if len(shards) > 0:
        drawn = shard_levels(key, dims, shards, -0.22, 0.18) * drawn
    return jnp.clip(drawn, min=-bound, max=bound).astype(kind)


def setup_inputs(seed: int = 0, part: int = 0) -> dict:
    keys = jax.random.split(jax.random.key(seed), 6)
    part_keys = jax.random.split(jax.random.fold_in(keys[5], part), 6)
    return {
        "s_matrix": scatter_about(part_keys[0], (NB, RY, 2 * RX), 1.0, 6.0, ((0, 2), (1, 8))),
        "beam_index": draw_beam_index(jax.random.fold_in(keys[5], 71), part),
        "beam_amp": jnp.clip(jnp.exp(math.log(2.0) - 1.3862944 * jax.random.uniform(keys[2], (NB,), jnp.float32) ** shard_levels(keys[2], (NB,), ((0, 2),), -0.2, 0.2)), 0.5, 2.0),
        "beam_phase": jnp.clip(jax.random.uniform(keys[3], (NB,), jnp.float32, -3.140625, 3.140625), -3.140625, 3.140625),
        "positions": with_ends(jax.random.randint(keys[4], (NBATCH, P_SIZE, 2), 0, RX), jax.random.fold_in(keys[4], 1), 0, RX - 1).astype(jnp.int32),
    }


def dft_tables():
    xs = jnp.arange(RX, dtype=jnp.int32)
    prod_x = jnp.mod(xs[:, None] * xs[None, :], RX).astype(jnp.float32)
    angle_x = 2.0 * math.pi / RX * prod_x
    cos_x = jnp.cos(angle_x) / math.sqrt(RX)
    sin_x = jnp.sin(angle_x) / math.sqrt(RX)
    table_x = jnp.concatenate([jnp.concatenate([cos_x, -sin_x], 1), jnp.concatenate([sin_x, cos_x], 1)], 0).astype(jnp.bfloat16)
    ys = jnp.arange(RY, dtype=jnp.int32)
    prod_y = jnp.mod(ys[:, None] * ys[None, :], RY).astype(jnp.float32)
    angle_y = 2.0 * math.pi / RY * prod_y
    table_y = jnp.concatenate([jnp.cos(angle_y), jnp.sin(angle_y)], 0) / math.sqrt(RY)
    return (table_x, table_y.astype(jnp.bfloat16))

def coefficients(spots, beam_index, beam_amp, beam_phase):
    rows_part = jnp.mod(spots[:, 0:1] * beam_index[None, :, 0], RY).astype(jnp.float32)
    cols_part = jnp.mod(spots[:, 1:2] * beam_index[None, :, 1], RX).astype(jnp.float32)
    theta = beam_phase[None, :] - 2.0 * math.pi * (rows_part / RY + cols_part / RX)
    scale = beam_amp[None, :] / math.sqrt(NB)
    return ((scale * jnp.cos(theta)).astype(jnp.bfloat16), (scale * jnp.sin(theta)).astype(jnp.bfloat16))

def reference(s_matrix, beam_index, beam_amp, beam_phase, positions):
    table_x, table_y = dft_tables()
    block = NB // N_BEAM
    results = []
    for batch in range(NBATCH):
        coef_re, coef_im = coefficients(positions[batch], beam_index, beam_amp, beam_phase)
        total = jnp.zeros((P_SIZE, RY, 2 * RX), jnp.float32)
        for part in range(N_BEAM):
            flat = s_matrix[part * block:(part + 1) * block].reshape(block, RY * 2 * RX)
            real_side = jnp.dot(coef_re[:, part * block:(part + 1) * block], flat, preferred_element_type=jnp.float32).reshape(P_SIZE, RY, 2 * RX)
            imag_side = jnp.dot(coef_im[:, part * block:(part + 1) * block], flat, preferred_element_type=jnp.float32).reshape(P_SIZE, RY, 2 * RX)
            wave_re = real_side[..., :RX] - imag_side[..., RX:]
            wave_im = real_side[..., RX:] + imag_side[..., :RX]
            rounded = lax.optimization_barrier(jnp.concatenate([wave_re, wave_im], -1).astype(jnp.bfloat16))
            total = total + rounded.astype(jnp.float32)
        wave = total.astype(jnp.bfloat16)
        half = jnp.dot(wave.reshape(P_SIZE * RY, 2 * RX), table_x, preferred_element_type=jnp.float32)
        half = half.astype(jnp.bfloat16).reshape(P_SIZE, RY, 2 * RX)
        spectrum = jnp.einsum('vy,pyc->pvc', table_y.astype(jnp.float32), half.astype(jnp.float32))
        spec_re = spectrum[:, :RY, :RX] + spectrum[:, RY:, RX:]
        spec_im = spectrum[:, :RY, RX:] - spectrum[:, RY:, :RX]
        results.append(spec_re * spec_re + spec_im * spec_im)
    return jnp.stack(results, 0)
```

```python
import functools
import math

import jax
import jax.numpy as jnp
from jax import lax
from jax.experimental import pallas as pl
from jax.experimental.pallas import tpu as pltpu
from jax.sharding import PartitionSpec as P


CHUNK = 8
TILE = 16
LANES = 128
SPAN = 64
NT = (((1,), (1,)), ((), ()))
F32 = jnp.float32
BF16 = jnp.bfloat16


def plain_tables(ry, rx):
    xs = jnp.arange(rx, dtype=jnp.int32)
    angle_x = 2.0 * math.pi / rx * jnp.mod(xs[:, None] * xs[None, :], rx).astype(F32)
    cos_x = jnp.cos(angle_x) / math.sqrt(rx)
    sin_x = jnp.sin(angle_x) / math.sqrt(rx)
    table_x = jnp.concatenate(
        [jnp.concatenate([cos_x, -sin_x], 1), jnp.concatenate([sin_x, cos_x], 1)], 0
    ).astype(BF16)
    ys = jnp.arange(ry, dtype=jnp.int32)
    angle_y = 2.0 * math.pi / ry * jnp.mod(ys[:, None] * ys[None, :], ry).astype(F32)
    table_y = jnp.concatenate([jnp.cos(angle_y), jnp.sin(angle_y)], 0) / math.sqrt(ry)
    return table_x, table_y.astype(BF16)


def plain_body(s_matrix, beam_index, beam_amp, beam_phase, positions):
    local_beams, local_rows, width = s_matrix.shape
    rx = width // 2
    n_space = lax.axis_size("space")
    n_beam = lax.axis_size("beam")
    ry = local_rows * n_space
    nb = local_beams * n_beam
    n_batch = positions.shape[0]
    per = positions.shape[1] // (n_space * n_beam)
    flat_s = s_matrix.reshape(local_beams, local_rows * width)
    table_x, table_y = plain_tables(ry, rx)

    def transform(wave, count):
        half = jnp.dot(wave.reshape(-1, width), table_x, preferred_element_type=F32)
        half = half.astype(BF16).reshape(-1, ry, width)
        spectrum = jnp.einsum("vy,pyc->pvc", table_y, half, preferred_element_type=F32)
        spec_re = spectrum[:, :ry, :rx] + spectrum[:, ry:, rx:]
        spec_im = spectrum[:, :ry, rx:] - spectrum[:, ry:, :rx]
        return (spec_re * spec_re + spec_im * spec_im).reshape(count, per, ry, rx)

    def one_group(chosen):
        count = chosen.shape[0]
        blocks = chosen.reshape(count, n_space, n_beam, per, 2)
        spots = jnp.transpose(blocks, (2, 1, 0, 3, 4)).reshape(-1, 2)
        rows_part = jnp.mod(spots[:, 0:1] * beam_index[None, :, 0], ry).astype(F32)
        cols_part = jnp.mod(spots[:, 1:2] * beam_index[None, :, 1], rx).astype(F32)
        theta = beam_phase[None, :] - 2.0 * math.pi * (rows_part / ry + cols_part / rx)
        scale = beam_amp[None, :] / math.sqrt(nb)
        coef = jnp.concatenate([scale * jnp.cos(theta), scale * jnp.sin(theta)], 0).astype(BF16)
        product = jnp.dot(coef, flat_s, preferred_element_type=F32)
        product = product.reshape(2, spots.shape[0], local_rows, width)
        wave_re = product[0, ..., :rx] - product[1, ..., rx:]
        wave_im = product[0, ..., rx:] + product[1, ..., :rx]
        rounded = lax.optimization_barrier(jnp.concatenate([wave_re, wave_im], -1).astype(BF16))
        summed = lax.psum_scatter(rounded, "beam", scatter_dimension=0, tiled=True)
        wave = lax.all_to_all(summed, "space", split_axis=0, concat_axis=1, tiled=True)
        return transform(wave, count)

    outputs = [one_group(positions[batch : batch + 1]) for batch in range(n_batch)]
    return jnp.concatenate(outputs, 0)


def split3(x):
    hi = x.astype(BF16)
    rest = x - hi.astype(F32)
    mid = rest.astype(BF16)
    lo = (rest - mid.astype(F32)).astype(BF16)
    return jnp.concatenate([hi, mid, lo], 1)


def coef_rows(halves, sizes, pos_ref, bidx_ref, amp_ref, phase_ref, a_ref):
    n_space, n_beam, per, ry, rx, nb = sizes
    me = lax.axis_index("beam")
    count = n_space * CHUNK
    probes = pos_ref.shape[2]
    beams = bidx_ref.shape[1]
    lane = lax.broadcasted_iota(jnp.int32, (1, LANES), 1)
    first = lane < SPAN
    index = (jnp.where(first, lane, lane - SPAN) - SPAN // 2).astype(F32)
    period = jnp.where(first, float(ry), float(rx))
    cosines, sines = [], []
    for chunk, mine in halves:
        owner = me if mine else n_beam - 1 - me
        batch, start = divmod(chunk * CHUNK, per)
        j = lax.broadcasted_iota(jnp.int32, (count, probes), 0)
        k = lax.broadcasted_iota(jnp.int32, (count, probes), 1)
        j_space = j // CHUNK
        mask = k == (j_space * n_beam + owner) * per + start + (j - j_space * CHUNK)
        spot = pos_ref[batch].astype(F32)
        row = jnp.sum(jnp.where(mask, spot[0:1], 0.0), axis=1, keepdims=True)
        col = jnp.sum(jnp.where(mask, spot[1:2], 0.0), axis=1, keepdims=True)
        turn = index * jnp.where(first, row, col)
        turn = turn - period * jnp.floor((turn + 0.5) / period)
        angle = turn * (2.0 * math.pi / period)
        cosines.append(jnp.cos(angle))
        sines.append(jnp.sin(angle))
    cosine = jnp.concatenate(cosines, 0)
    sine = jnp.concatenate(sines, 0)
    table = jnp.concatenate(
        [
            split3(jnp.where(first, cosine, 0.0)),
            split3(jnp.where(first, sine, 0.0)),
            split3(jnp.where(first, 0.0, cosine)),
            split3(jnp.where(first, 0.0, sine)),
        ],
        0,
    )
    r = lax.broadcasted_iota(jnp.int32, (LANES, beams), 0)
    want = jnp.where(
        r < SPAN, bidx_ref[0:1, :] + SPAN // 2, bidx_ref[1:2, :] + (SPAN + SPAN // 2)
    )
    pick = jnp.where(r == want, 1.0, 0.0).astype(BF16)
    chosen = jnp.dot(table, jnp.concatenate([pick] * 3, 0), preferred_element_type=F32)
    n = count * len(halves)
    row_re, row_im = chosen[:n], -chosen[n : 2 * n]
    col_re, col_im = chosen[2 * n : 3 * n], -chosen[3 * n :]
    both_re = row_re * col_re - row_im * col_im
    both_im = row_re * col_im + row_im * col_re
    scale = amp_ref[...] / math.sqrt(nb)
    beam_re = scale * jnp.cos(phase_ref[...])
    beam_im = scale * jnp.sin(phase_ref[...])
    coef_re = (beam_re * both_re - beam_im * both_im).astype(BF16)
    coef_im = (beam_re * both_im + beam_im * both_re).astype(BF16)
    for h in range(len(halves)):
        part = slice(h * count, (h + 1) * count)
        real = slice(2 * h * count, (2 * h + 1) * count)
        imag = slice((2 * h + 1) * count, (2 * h + 2) * count)
        a_ref[real, :beams] = coef_re[part]
        a_ref[real, beams:] = -coef_im[part]
        a_ref[imag, :beams] = coef_im[part]
        a_ref[imag, beams:] = coef_re[part]


def pack_blocks(out_refs, low_ref, high_ref, n_space, rows, rx):
    me = lax.axis_index("space")
    count = n_space * CHUNK
    stride = 2 * count
    units = CHUNK * rows // TILE
    tail = rx - LANES
    hole = LANES - tail
    lane = lax.broadcasted_iota(jnp.int32, (TILE, LANES), 1)
    for d, out_ref in enumerate(out_refs):
        space = me ^ d
        for plane in range(2):
            base = plane * count + space * CHUNK
            at = plane * 2 * LANES

            def unit(ref, n):
                probe, block = divmod(n, rows // TILE)
                begin = block * TILE * stride + base + probe
                return ref[pl.ds(begin, TILE, stride=stride), :]

            last_low = unit(low_ref, units - 1)
            last_high = unit(high_ref, units - 1)
            for n in range(units - 1):
                begin = n * hole
                source = last_low if begin < LANES else last_high
                piece = pltpu.roll(source, (tail - begin) % LANES, 1)
                high = jnp.where(lane < tail, unit(high_ref, n), piece)
                out_ref[n, :, at : at + LANES] = unit(low_ref, n).astype(BF16)
                out_ref[n, :, at + LANES : at + 2 * LANES] = high.astype(BF16)


def wave_kernel(theirs, mine, sizes, rows, step_rows, *refs):
    n_space, n_beam, per, ry, rx, nb = sizes
    pos_ref, bidx_ref, amp_ref, phase_ref, s_ref = refs[:5]
    refs = refs[5:]
    recv_ref = sent_ref = None
    if mine is not None:
        recv_ref, refs = refs[0], refs[1:]
    if theirs is not None:
        sent_ref, refs = refs[0], refs[1:]
    out_refs = ()
    if mine is not None:
        out_refs, refs = refs[:n_space], refs[n_space:]
        low_ref, high_ref = refs[1:3]
    a_ref = refs[0]
    step = pl.program_id(0)
    halves = []
    if theirs is not None:
        halves.append((theirs, False))
    if mine is not None:
        halves.append((mine, True))
    block = 2 * n_space * CHUNK
    beams = s_ref.shape[2]

    @pl.when(step == 0)
    def _():
        coef_rows(halves, sizes, pos_ref, bidx_ref, amp_ref, phase_ref, a_ref)

    for i in range(step_rows):
        part = lax.dot_general(
            a_ref[:, :beams], s_ref[i, :rx, :], NT, preferred_element_type=F32
        ) + lax.dot_general(a_ref[:, beams:], s_ref[i, rx:, :], NT, preferred_element_type=F32)
        if theirs is not None:
            sent_ref[i] = part[:block].astype(BF16)
        if mine is not None:
            total = part[-block:] + recv_ref[i].astype(F32)
            at = pl.multiple_of((step * step_rows + i) * block, block)
            low_ref[pl.ds(at, block), :] = total[:, :LANES]
            high_ref[pl.ds(at, block), : rx - LANES] = total[:, LANES:]

    if mine is not None:

        @pl.when(step == pl.num_programs(0) - 1)
        def _():
            pack_blocks(out_refs, low_ref, high_ref, n_space, rows, rx)


def wave_call(theirs, mine, sizes, pos, bidx, amp, phase, s_rows, recv):
    n_space, n_beam, per, ry, rx, nb = sizes
    rows, width, beams = s_rows.shape
    step_rows = 4
    block = 2 * n_space * CHUNK
    n_half = (theirs is not None) + (mine is not None)
    units = CHUNK * rows // TILE

    def whole(a):
        return pl.BlockSpec(a.shape, lambda i: (0,) * a.ndim)

    in_specs = [whole(pos), whole(bidx), whole(amp), whole(phase)]
    in_specs.append(pl.BlockSpec((step_rows, width, beams), lambda i: (i, 0, 0)))
    args = [pos, bidx, amp, phase, s_rows]
    out_shapes, out_specs = [], []
    scratch = [pltpu.VMEM((n_half * block, 2 * beams), BF16)]
    row_spec = pl.BlockSpec((step_rows, block, rx), lambda i: (i, 0, 0))
    if mine is not None:
        in_specs.append(row_spec)
        args.append(recv)
    if theirs is not None:
        out_shapes.append(jax.ShapeDtypeStruct((rows, block, rx), BF16))
        out_specs.append(row_spec)
    if mine is not None:
        wire = (units - 1, TILE, 4 * LANES)
        for _ in range(n_space):
            out_shapes.append(jax.ShapeDtypeStruct(wire, BF16))
            out_specs.append(pl.BlockSpec(wire, lambda i: (0, 0, 0)))
        scratch += [pltpu.VMEM((rows * block, LANES), F32)] * 2
    flops = 2 * n_half * block * rows * width * beams
    out = pl.pallas_call(
        functools.partial(wave_kernel, theirs, mine, sizes, rows, step_rows),
        grid=(rows // step_rows,),
        in_specs=in_specs,
        out_specs=out_specs,
        out_shape=out_shapes,
        scratch_shapes=scratch,
        cost_estimate=pl.CostEstimate(
            flops=flops, bytes_accessed=2 * rows * width * beams, transcendentals=0
        ),
        compiler_params=pltpu.CompilerParams(vmem_limit_bytes=48 << 20),
        name="wave",
    )(*args)
    out = list(out)
    sent = out.pop(0) if theirs is not None else None
    return sent, out


def transform_kernel(n_space, rows, rx, ry, *refs):
    blocks = refs[:n_space]
    ty_ref, tx_ref = refs[n_space : n_space + 2]
    out_ref, w_ref = refs[-2:]
    p = pl.program_id(0)
    per_probe = rows // TILE
    units = CHUNK * per_probe
    tail = rx - LANES
    hole = LANES - tail
    plane = 2 * LANES

    for d in range(n_space):
        for b in range(per_probe):
            row = d * rows + b * TILE
            last = b == per_probe - 1
            n = p * per_probe + b
            if last:
                n = jnp.minimum(n, units - 2)
            w_ref[row : row + TILE, :] = blocks[d][n]

    @pl.when(p == CHUNK - 1)
    def _():
        lane = lax.broadcasted_iota(jnp.int32, (TILE, LANES), 1)
        for d in range(n_space):
            row = d * rows + (per_probe - 1) * TILE
            for half in range(2):
                low = jnp.zeros((TILE, LANES), F32)
                high = jnp.zeros((TILE, LANES), F32)
                for n in range(units - 1):
                    begin = n * hole
                    piece = blocks[d][n, :, half * plane + LANES : (half + 1) * plane].astype(F32)
                    piece = pltpu.roll(piece, (begin - tail) % LANES, 1)
                    inside = (lane >= begin % LANES) & (lane < begin % LANES + hole)
                    if begin < LANES:
                        low = jnp.where(inside, piece, low)
                    else:
                        high = jnp.where(inside, piece, high)
                at = half * plane
                w_ref[row : row + TILE, at : at + LANES] = low.astype(BF16)
                w_ref[row : row + TILE, at + LANES : at + plane] = high.astype(BF16)

    w = w_ref[...]
    both = jnp.dot(ty_ref[...], w, preferred_element_type=F32)
    g_re = both[:ry, :plane] + both[ry:, plane:]
    g_im = both[:ry, plane:] - both[ry:, :plane]
    g = jnp.concatenate([g_re.astype(BF16), g_im.astype(BF16)], 1)
    spec = lax.dot_general(tx_ref[...], g, NT, preferred_element_type=F32)
    re, im = spec[:rx], spec[rx:]
    out_ref[0] = re * re + im * im


def transform_call(chunk, blocks, table_y, table_x, out, n_local, rows, rx, ry):
    n_space = len(blocks)

    def whole(a):
        return pl.BlockSpec(a.shape, lambda i: (0,) * a.ndim)

    args = [*blocks, table_y, table_x]
    in_specs = [whole(a) for a in args]
    aliases = {}
    if out is not None:
        aliases = {len(args): 0}
        args.append(out)
        in_specs.append(pl.BlockSpec(memory_space=pl.ANY))
    flops = 2 * CHUNK * (2 * ry * ry * 4 * LANES + 2 * rx * 4 * LANES * ry)
    return pl.pallas_call(
        functools.partial(transform_kernel, n_space, rows, rx, ry),
        grid=(CHUNK,),
        in_specs=in_specs,
        out_specs=pl.BlockSpec((1, rx, ry), lambda i: (chunk * CHUNK + i, 0, 0)),
        out_shape=jax.ShapeDtypeStruct((n_local, rx, ry), F32),
        scratch_shapes=[pltpu.VMEM((ry, 4 * LANES), BF16)],
        input_output_aliases=aliases,
        cost_estimate=pl.CostEstimate(
            flops=flops, bytes_accessed=CHUNK * rx * ry * 6, transcendentals=0
        ),
        compiler_params=pltpu.CompilerParams(vmem_limit_bytes=32 << 20),
        name="transform",
    )(*args)


def wire_tables(rows, n_space, rx, ry):
    me = lax.axis_index("space")
    order = jnp.arange(n_space, dtype=jnp.int32) ^ me
    ys = (order[:, None] * rows + jnp.arange(rows, dtype=jnp.int32)[None, :]).reshape(-1)
    vs = jnp.arange(ry, dtype=jnp.int32)
    angle_y = 2.0 * math.pi / ry * jnp.mod(vs[:, None] * ys[None, :], ry).astype(F32)
    table_y = jnp.concatenate([jnp.cos(angle_y), jnp.sin(angle_y)], 0) / math.sqrt(ry)
    xs = jnp.arange(rx, dtype=jnp.int32)
    angle_x = 2.0 * math.pi / rx * jnp.mod(xs[:, None] * xs[None, :], rx).astype(F32)
    pad = ((0, 0), (0, 2 * LANES - rx))
    cos_x = jnp.pad(jnp.cos(angle_x) / math.sqrt(rx), pad)
    sin_x = jnp.pad(jnp.sin(angle_x) / math.sqrt(rx), pad)
    table_x = jnp.concatenate(
        [jnp.concatenate([cos_x, sin_x], 1), jnp.concatenate([-sin_x, cos_x], 1)], 0
    )
    return table_y.astype(BF16), table_x.astype(BF16)


def wire_body(s_matrix, beam_index, beam_amp, beam_phase, positions):
    beams, rows, width = s_matrix.shape
    rx = width // 2
    n_space = lax.axis_size("space")
    n_beam = lax.axis_size("beam")
    ry = rows * n_space
    n_batch, probes = positions.shape[:2]
    per = probes // (n_space * n_beam)
    n_local = n_batch * per
    n_chunk = n_local // CHUNK
    sizes = (n_space, n_beam, per, ry, rx, beams * n_beam)
    s_rows = jnp.transpose(s_matrix, (1, 2, 0))
    pos = jnp.transpose(positions, (0, 2, 1))
    bidx = beam_index.T
    amp = beam_amp.reshape(1, beams)
    phase = beam_phase.reshape(1, beams)
    swap = [(i, n_beam - 1 - i) for i in range(n_beam)]

    out = None
    recv = None
    arrived = []
    for i in range(n_chunk + 1):
        theirs = i if i < n_chunk else None
        mine = i - 1 if i > 0 else None
        sent, packed = wave_call(theirs, mine, sizes, pos, bidx, amp, phase, s_rows, recv)
        if theirs is not None:
            recv = lax.ppermute(sent, "beam", swap)
        if mine is not None:
            blocks = [packed[0]]
            for d in range(1, n_space):
                pairs = [(k, k ^ d) for k in range(n_space)]
                blocks.append(lax.ppermute(packed[d], "space", pairs))
            arrived.append(blocks)
    table_y, table_x = wire_tables(rows, n_space, rx, ry)
    for chunk in range(n_chunk):
        out = transform_call(chunk, arrived[chunk], table_y, table_x, out, n_local, rows, rx, ry)
    out = jnp.transpose(out, (0, 2, 1))
    return out.reshape(n_batch, per, ry, rx)


def fits(s_shape, probes, mesh):
    n_space, n_beam = mesh.shape["space"], mesh.shape["beam"]
    rows = s_shape[1] // n_space
    rx = s_shape[2] // 2
    beams = s_shape[0] // (mesh.shape["groups"] * n_beam)
    per = probes // (n_space * n_beam)
    units = CHUNK * rows // TILE
    return (
        n_beam == 2
        and n_space & (n_space - 1) == 0
        and per % CHUNK == 0
        and rows % TILE == 0
        and beams % LANES == 0
        and LANES < rx < 2 * LANES
        and (units - 1) * (2 * LANES - rx) == rx
        and LANES % (2 * LANES - rx) == 0
        and (rows * n_space) % LANES == 0
    )


def solution(mesh):
    in_specs = (P(("groups", "beam"), "space", None), P("beam", None), P("beam"), P("beam"), P())
    out_specs = P("groups", ("space", "beam"), None, None)

    def program(s_matrix, beam_index, beam_amp, beam_phase, positions):
        body = wire_body if fits(s_matrix.shape, positions.shape[1], mesh) else plain_body
        mapped = jax.shard_map(
            body, mesh=mesh, in_specs=in_specs, out_specs=out_specs, check_vma=False
        )
        return mapped(s_matrix, beam_index, beam_amp, beam_phase, positions)

    return program
```

```python
import functools
import math

import jax
import jax.numpy as jnp
from jax import lax
from jax.experimental import pallas as pl
from jax.experimental.pallas import tpu as pltpu
from jax.sharding import PartitionSpec as P


OCT = 8
TILE = 16
UNITS = 2 * OCT
STEP_ROWS = 4
STEP_PROBES = 2
LANES = 128
SPAN = 64
NT = (((1,), (1,)), ((), ()))
F32 = jnp.float32
BF16 = jnp.bfloat16


def plain_tables(ry, rx):
    xs = jnp.arange(rx, dtype=jnp.int32)
    angle_x = 2.0 * math.pi / rx * jnp.mod(xs[:, None] * xs[None, :], rx).astype(F32)
    cos_x = jnp.cos(angle_x) / math.sqrt(rx)
    sin_x = jnp.sin(angle_x) / math.sqrt(rx)
    table_x = jnp.concatenate(
        [jnp.concatenate([cos_x, -sin_x], 1), jnp.concatenate([sin_x, cos_x], 1)], 0
    ).astype(BF16)
    ys = jnp.arange(ry, dtype=jnp.int32)
    angle_y = 2.0 * math.pi / ry * jnp.mod(ys[:, None] * ys[None, :], ry).astype(F32)
    table_y = jnp.concatenate([jnp.cos(angle_y), jnp.sin(angle_y)], 0) / math.sqrt(ry)
    return table_x, table_y.astype(BF16)


def plain_body(s_matrix, beam_index, beam_amp, beam_phase, positions):
    local_beams, local_rows, width = s_matrix.shape
    rx = width // 2
    n_space = lax.axis_size("space")
    n_beam = lax.axis_size("beam")
    ry = local_rows * n_space
    nb = local_beams * n_beam
    n_batch = positions.shape[0]
    per = positions.shape[1] // (n_space * n_beam)
    flat_s = s_matrix.reshape(local_beams, local_rows * width)
    table_x, table_y = plain_tables(ry, rx)

    def transform(wave, count):
        half = jnp.dot(wave.reshape(-1, width), table_x, preferred_element_type=F32)
        half = half.astype(BF16).reshape(-1, ry, width)
        spectrum = jnp.einsum("vy,pyc->pvc", table_y, half, preferred_element_type=F32)
        spec_re = spectrum[:, :ry, :rx] + spectrum[:, ry:, rx:]
        spec_im = spectrum[:, :ry, rx:] - spectrum[:, ry:, :rx]
        return (spec_re * spec_re + spec_im * spec_im).reshape(count, per, ry, rx)

    def one_group(chosen):
        count = chosen.shape[0]
        blocks = chosen.reshape(count, n_space, n_beam, per, 2)
        spots = jnp.transpose(blocks, (2, 1, 0, 3, 4)).reshape(-1, 2)
        rows_part = jnp.mod(spots[:, 0:1] * beam_index[None, :, 0], ry).astype(F32)
        cols_part = jnp.mod(spots[:, 1:2] * beam_index[None, :, 1], rx).astype(F32)
        theta = beam_phase[None, :] - 2.0 * math.pi * (rows_part / ry + cols_part / rx)
        scale = beam_amp[None, :] / math.sqrt(nb)
        coef = jnp.concatenate([scale * jnp.cos(theta), scale * jnp.sin(theta)], 0).astype(BF16)
        product = jnp.dot(coef, flat_s, preferred_element_type=F32)
        product = product.reshape(2, spots.shape[0], local_rows, width)
        wave_re = product[0, ..., :rx] - product[1, ..., rx:]
        wave_im = product[0, ..., rx:] + product[1, ..., :rx]
        rounded = lax.optimization_barrier(jnp.concatenate([wave_re, wave_im], -1).astype(BF16))
        summed = lax.psum_scatter(rounded, "beam", scatter_dimension=0, tiled=True)
        wave = lax.all_to_all(summed, "space", split_axis=0, concat_axis=1, tiled=True)
        return transform(wave, count)

    outputs = [one_group(positions[batch : batch + 1]) for batch in range(n_batch)]
    return jnp.concatenate(outputs, 0)


def split3(x):
    hi = x.astype(BF16)
    rest = x - hi.astype(F32)
    mid = rest.astype(BF16)
    lo = (rest - mid.astype(F32)).astype(BF16)
    return jnp.concatenate([hi, mid, lo], 1)


def coef_matrix(halves, sizes, pos_ref, bidx_ref, amp_ref, phase_ref, at_ref):
    n_space, n_beam, per, ry, rx, nb = sizes
    me = lax.axis_index("beam")
    count = n_space * OCT
    probes = pos_ref.shape[2]
    beams = bidx_ref.shape[1]
    lane = lax.broadcasted_iota(jnp.int32, (1, LANES), 1)
    first = lane < SPAN
    index = (jnp.where(first, lane, lane - SPAN) - SPAN // 2).astype(F32)
    period = jnp.where(first, float(ry), float(rx))
    cosines, sines = [], []
    for octet, mine in halves:
        owner = me if mine else n_beam - 1 - me
        batch, start = divmod(octet * OCT, per)
        j = lax.broadcasted_iota(jnp.int32, (count, probes), 0)
        k = lax.broadcasted_iota(jnp.int32, (count, probes), 1)
        j_space = j // OCT
        mask = k == (j_space * n_beam + owner) * per + start + (j - j_space * OCT)
        spot = pos_ref[batch].astype(F32)
        row = jnp.sum(jnp.where(mask, spot[0:1], 0.0), axis=1, keepdims=True)
        col = jnp.sum(jnp.where(mask, spot[1:2], 0.0), axis=1, keepdims=True)
        turn = index * jnp.where(first, row, col)
        turn = turn - period * jnp.floor((turn + 0.5) / period)
        angle = turn * (2.0 * math.pi / period)
        cosines.append(jnp.cos(angle))
        sines.append(jnp.sin(angle))
    cosine = jnp.concatenate(cosines, 0)
    sine = jnp.concatenate(sines, 0)
    table = jnp.concatenate(
        [
            split3(jnp.where(first, cosine, 0.0)),
            split3(jnp.where(first, sine, 0.0)),
            split3(jnp.where(first, 0.0, cosine)),
            split3(jnp.where(first, 0.0, sine)),
        ],
        0,
    )
    r = lax.broadcasted_iota(jnp.int32, (LANES, beams), 0)
    want = jnp.where(
        r < SPAN, bidx_ref[0:1, :] + SPAN // 2, bidx_ref[1:2, :] + (SPAN + SPAN // 2)
    )
    pick = jnp.where(r == want, 1.0, 0.0).astype(BF16)
    chosen = jnp.dot(table, jnp.concatenate([pick] * 3, 0), preferred_element_type=F32)
    n = count * len(halves)
    row_re, row_im = chosen[:n], -chosen[n : 2 * n]
    col_re, col_im = chosen[2 * n : 3 * n], -chosen[3 * n :]
    both_re = row_re * col_re - row_im * col_im
    both_im = row_re * col_im + row_im * col_re
    scale = amp_ref[...] / math.sqrt(nb)
    beam_re = scale * jnp.cos(phase_ref[...])
    beam_im = scale * jnp.sin(phase_ref[...])
    coef_re = beam_re * both_re - beam_im * both_im
    coef_im = beam_re * both_im + beam_im * both_re
    for h in range(len(halves)):
        part = slice(h * count, (h + 1) * count)
        re, im = coef_re[part], coef_im[part]
        lanes = slice(2 * h * count, 2 * (h + 1) * count)
        at_ref[:beams, lanes] = jnp.concatenate([re, im], 0).T.astype(BF16)
        at_ref[beams:, lanes] = jnp.concatenate([-im, re], 0).T.astype(BF16)


def wave_kernel(octets, sizes, pos_ref, bidx_ref, amp_ref, phase_ref, s_ref, sent_ref, kept_ref, at_ref):
    rx = sizes[4]
    step_rows, _, _ = s_ref.shape
    half = sent_ref.shape[2]

    @pl.when(pl.program_id(0) == 0)
    def _():
        halves = [(o, False) for o in octets] + [(o, True) for o in octets]
        coef_matrix(halves, sizes, pos_ref, bidx_ref, amp_ref, phase_ref, at_ref)

    for i in range(step_rows):
        both = jnp.concatenate([s_ref[i, :rx, :], s_ref[i, rx:, :]], 1)
        part = jnp.dot(both, at_ref[...], preferred_element_type=F32).astype(BF16)
        sent_ref[i] = part[:, :half]
        kept_ref[i] = part[:, half:]


def whole(a):
    return pl.BlockSpec(a.shape, lambda i: (0,) * a.ndim)


def wave_call(octets, tiles, sizes, pos, bidx, amp, phase, s_rows):
    n_space, _, _, _, rx, _ = sizes
    width, beams = s_rows.shape[1:]
    rows = len(tiles) * TILE
    begin = tiles[0] * TILE // STEP_ROWS
    half = len(octets) * 2 * n_space * OCT
    row_spec = pl.BlockSpec((STEP_ROWS, rx, half), lambda i: (i, 0, 0))
    return pl.pallas_call(
        functools.partial(wave_kernel, octets, sizes),
        grid=(rows // STEP_ROWS,),
        in_specs=[
            whole(pos),
            whole(bidx),
            whole(amp),
            whole(phase),
            pl.BlockSpec((STEP_ROWS, width, beams), lambda i: (begin + i, 0, 0)),
        ],
        out_specs=[row_spec] * 2,
        out_shape=[jax.ShapeDtypeStruct((rows, rx, half), BF16)] * 2,
        scratch_shapes=[pltpu.VMEM((2 * beams, 2 * half), BF16)],
        cost_estimate=pl.CostEstimate(
            flops=4 * half * rows * width * beams,
            bytes_accessed=2 * rows * width * (beams + half),
            transcendentals=0,
        ),
        compiler_params=pltpu.CompilerParams(vmem_limit_bytes=40 << 20),
        name="wave",
    )(pos, bidx, amp, phase, s_rows)


def pack_kernel(n_octet, n_space, kept_ref, recv_ref, *refs):
    out_refs, (low_ref, high_ref) = refs[:n_space], refs[n_space:]
    me = lax.axis_index("space")
    rx = kept_ref.shape[1]
    count = n_space * OCT
    stride = n_octet * 2 * count
    tail = rx - LANES
    hole = LANES - tail
    lane = lax.broadcasted_iota(jnp.int32, (TILE, LANES), 1)
    for i in range(TILE):
        total = (kept_ref[i].astype(F32) + recv_ref[i].astype(F32)).T
        low_ref[i * stride : (i + 1) * stride, :] = total[:, :LANES]
        high_ref[i * stride : (i + 1) * stride, :tail] = total[:, LANES:]
    for octet in range(n_octet):
        for d, out_ref in enumerate(out_refs):
            base = octet * 2 * count + (me ^ d) * OCT

            def unit(ref, m):
                probe, plane = divmod(m, 2)
                return ref[pl.ds(base + plane * count + probe, TILE, stride=stride), :]

            last_low = unit(low_ref, UNITS - 1)
            last_high = unit(high_ref, UNITS - 1)
            for m in range(UNITS - 1):
                begin = m * hole
                source = last_low if begin < LANES else last_high
                piece = pltpu.roll(source, (tail - begin) % LANES, 1)
                high = jnp.where(lane < tail, unit(high_ref, m), piece)
                n = octet * (UNITS - 1) + m
                out_ref[n, :, :LANES] = unit(low_ref, m).astype(BF16)
                out_ref[n, :, LANES:] = high.astype(BF16)


def pack_call(n_octet, n_space, kept, recv):
    rows, rx, half = kept.shape
    in_spec = pl.BlockSpec((TILE, rx, half), lambda i: (i, 0, 0))
    wire = (n_octet * (UNITS - 1), TILE, 2 * LANES)
    out_shape = jax.ShapeDtypeStruct((rows // TILE * wire[0], *wire[1:]), BF16)
    return pl.pallas_call(
        functools.partial(pack_kernel, n_octet, n_space),
        grid=(rows // TILE,),
        in_specs=[in_spec] * 2,
        out_specs=[pl.BlockSpec(wire, lambda i: (i, 0, 0))] * n_space,
        out_shape=[out_shape] * n_space,
        scratch_shapes=[pltpu.VMEM((TILE * half, LANES), F32)] * 2,
        cost_estimate=pl.CostEstimate(
            flops=rows * rx * half, bytes_accessed=6 * rows * rx * half, transcendentals=0
        ),
        compiler_params=pltpu.CompilerParams(vmem_limit_bytes=24 << 20),
        name="pack",
    )(kept, recv)


def transform_kernel(n_space, n_tile, rx, ry, *refs):
    count = n_space * n_tile
    blocks = refs[:count]
    ty_ref, tx_ref = refs[count : count + 2]
    out_ref, w_ref = refs[-2:]
    step = pl.program_id(0)
    tail = rx - LANES
    hole = LANES - tail
    last = UNITS - 1

    for q in range(STEP_PROBES):
        p = step * STEP_PROBES + q
        for b in range(count):
            row = b * TILE
            w_ref[q, row : row + TILE, :] = blocks[b][2 * p]
            w_ref[q, ry + row : ry + row + TILE, :] = blocks[b][jnp.minimum(2 * p + 1, last - 1)]

    @pl.when(step == pl.num_programs(0) - 1)
    def _():
        lane = lax.broadcasted_iota(jnp.int32, (TILE, LANES), 1)
        for b in range(count):
            row = ry + b * TILE
            halves = [jnp.zeros((TILE, LANES), F32)] * 2
            for n in range(last):
                which, begin = divmod(n * hole, LANES)
                piece = blocks[b][n, :, LANES:].astype(F32)
                piece = pltpu.roll(piece, (begin - tail) % LANES, 1)
                inside = (lane >= begin) & (lane < begin + hole)
                halves[which] = jnp.where(inside, piece, halves[which])
            w_ref[STEP_PROBES - 1, row : row + TILE, :LANES] = halves[0].astype(BF16)
            w_ref[STEP_PROBES - 1, row : row + TILE, LANES:] = halves[1].astype(BF16)

    for q in range(STEP_PROBES):
        g = jnp.dot(ty_ref[...], w_ref[q], preferred_element_type=F32).astype(BF16)
        g = jnp.concatenate([g[:ry], g[ry:]], 1)
        spec = lax.dot_general(tx_ref[...], g, NT, preferred_element_type=F32)
        re, im = spec[:rx], spec[rx:]
        out_ref[q] = re * re + im * im


def transform_call(octet, sources, table_y, table_x, out, n_local, n_space, rx, ry):
    group = (UNITS - 1, TILE, 2 * LANES)
    args = [a for a, _ in sources] + [table_y, table_x]
    in_specs = [pl.BlockSpec(group, lambda i, g=g: (g, 0, 0)) for _, g in sources]
    in_specs += [whole(table_y), whole(table_x)]
    aliases = {}
    if out is not None:
        aliases = {len(args): 0}
        args.append(out)
        in_specs.append(pl.BlockSpec(memory_space=pl.ANY))
    steps = OCT // STEP_PROBES
    return pl.pallas_call(
        functools.partial(transform_kernel, n_space, len(sources) // n_space, rx, ry),
        grid=(steps,),
        in_specs=in_specs,
        out_specs=pl.BlockSpec((STEP_PROBES, rx, ry), lambda i: (octet * steps + i, 0, 0)),
        out_shape=jax.ShapeDtypeStruct((n_local, rx, ry), F32),
        scratch_shapes=[pltpu.VMEM((STEP_PROBES, 2 * ry, 2 * LANES), BF16)],
        input_output_aliases=aliases,
        cost_estimate=pl.CostEstimate(
            flops=OCT * 2 * (4 * ry * ry + 4 * rx * ry) * 2 * LANES,
            bytes_accessed=OCT * rx * ry * 8,
            transcendentals=0,
        ),
        compiler_params=pltpu.CompilerParams(vmem_limit_bytes=24 << 20),
        name="transform",
    )(*args)


def wire_tables(rows, n_space, rx, ry):
    me = lax.axis_index("space")
    order = jnp.arange(n_space, dtype=jnp.int32) ^ me
    ys = (order[:, None] * rows + jnp.arange(rows, dtype=jnp.int32)[None, :]).reshape(-1)
    vs = jnp.arange(ry, dtype=jnp.int32)
    angle_y = 2.0 * math.pi / ry * jnp.mod(vs[:, None] * ys[None, :], ry).astype(F32)
    cos_y = (jnp.cos(angle_y) / math.sqrt(ry)).astype(BF16)
    sin_y = (jnp.sin(angle_y) / math.sqrt(ry)).astype(BF16)
    table_y = jnp.concatenate(
        [jnp.concatenate([cos_y, sin_y], 1), jnp.concatenate([-sin_y, cos_y], 1)], 0
    )
    xs = jnp.arange(rx, dtype=jnp.int32)
    angle_x = 2.0 * math.pi / rx * jnp.mod(xs[:, None] * xs[None, :], rx).astype(F32)
    pad = ((0, 0), (0, 2 * LANES - rx))
    cos_x = jnp.pad(jnp.cos(angle_x) / math.sqrt(rx), pad)
    sin_x = jnp.pad(jnp.sin(angle_x) / math.sqrt(rx), pad)
    table_x = jnp.concatenate(
        [jnp.concatenate([cos_x, sin_x], 1), jnp.concatenate([-sin_x, cos_x], 1)], 0
    )
    return table_y, table_x.astype(BF16)


def plan(n_octet, n_tile):
    every = tuple(range(n_tile))
    pieces = [((0,), (t,)) for t in every]
    o = 1
    while o < n_octet:
        size = 2 if 2 <= o and o + 2 < n_octet else 1
        pieces.append((tuple(range(o, o + size)), every))
        o += size
    return pieces


def wire_body(s_matrix, beam_index, beam_amp, beam_phase, positions):
    beams, rows, width = s_matrix.shape
    rx = width // 2
    n_space = lax.axis_size("space")
    n_beam = lax.axis_size("beam")
    ry = rows * n_space
    n_batch, probes = positions.shape[:2]
    per = probes // (n_space * n_beam)
    n_local = n_batch * per
    n_octet = n_local // OCT
    n_tile = rows // TILE
    sizes = (n_space, n_beam, per, ry, rx, beams * n_beam)
    s_rows = jnp.transpose(s_matrix, (1, 2, 0))
    pos = jnp.transpose(positions, (0, 2, 1))
    bidx = beam_index.T
    amp = beam_amp.reshape(1, beams)
    phase = beam_phase.reshape(1, beams)
    swap = [(i, n_beam - 1 - i) for i in range(n_beam)]

    found = {}
    for octets, tiles in plan(n_octet, n_tile):
        sent, kept = wave_call(octets, tiles, sizes, pos, bidx, amp, phase, s_rows)
        recv = lax.ppermute(sent, "beam", swap)
        blocks = list(pack_call(len(octets), n_space, kept, recv))
        for d in range(1, n_space):
            pairs = [(k, k ^ d) for k in range(n_space)]
            blocks[d] = lax.ppermute(blocks[d], "space", pairs)
        for ti, tile in enumerate(tiles):
            for oi, octet in enumerate(octets):
                for d in range(n_space):
                    found[octet, d, tile] = (blocks[d], ti * len(octets) + oi)
    table_y, table_x = wire_tables(rows, n_space, rx, ry)
    out = None
    for octet in range(n_octet):
        sources = [found[octet, d, t] for d in range(n_space) for t in range(n_tile)]
        out = transform_call(octet, sources, table_y, table_x, out, n_local, n_space, rx, ry)
    return jnp.transpose(out, (0, 2, 1)).reshape(n_batch, per, ry, rx)


def fits(s_shape, n_batch, probes, mesh):
    n_space, n_beam = mesh.shape["space"], mesh.shape["beam"]
    rows = s_shape[1] // n_space
    rx = s_shape[2] // 2
    beams = s_shape[0] // (mesh.shape["groups"] * n_beam)
    per = probes // (n_space * n_beam)
    hole = 2 * LANES - rx
    return (
        n_beam == 2
        and n_space >= 2
        and n_space & (n_space - 1) == 0
        and per % OCT == 0
        and n_batch * per // OCT >= 2
        and rows % TILE == 0
        and beams % LANES == 0
        and LANES < rx < 2 * LANES
        and (UNITS - 1) * hole == rx
        and LANES % hole == 0
        and (2 * n_space * OCT) % LANES == 0
        and (rows * n_space) % LANES == 0
    )


def solution(mesh):
    in_specs = (P(("groups", "beam"), "space", None), P("beam", None), P("beam"), P("beam"), P())
    out_specs = P("groups", ("space", "beam"), None, None)

    def mapped(body):
        return jax.shard_map(
            body, mesh=mesh, in_specs=in_specs, out_specs=out_specs, check_vma=False
        )

    def program(s_matrix, beam_index, beam_amp, beam_phase, positions):
        n_batch, probes = positions.shape[:2]
        args = (s_matrix, beam_index, beam_amp, beam_phase, positions)
        if not fits(s_matrix.shape, n_batch, probes, mesh):
            return mapped(plain_body)(*args)
        return mapped(wire_body)(*args)

    return program
```
